1024 devices in a mesh: ctx: 64 (over x, y_lo, core), head: 16 (over z, y_hi).
Axes of the slice: x: 8, y: 8 (y_hi: 2, y_lo: 4; y = y_hi * 4 + y_lo), z: 8, core: 2. Of those that a mesh axis runs over, the one named last changes fastest.
Arguments:
- query: bfloat16 [16, 8192, 2048], P('head', 'ctx'), as said below
- key: bfloat16 [16, 8192, 512], P('head', 'ctx'), as said below
- value: bfloat16 [16, 8192, 512], P('head', 'ctx'), may hold values from -6 to 6
- attn_out: bfloat16 [16, 8192, 2048], P(None, 'ctx', 'head'), may hold values from -6 to 6
- grad_out: bfloat16 [16, 8192, 2048], P('head', 'ctx'), may hold values from -24 to 24
- logsumexp: float32 [16, 8192, 16], P(None, 'ctx', 'head'), as said below
- span_order: int32 [128], replicated, may hold values from 0 to 127, as said below
Outputs:
- grad_query: bfloat16 [16, 8192, 2048], P('head', 'ctx')
- grad_key: bfloat16 [16, 8192, 512], P('head', 'ctx')
- grad_value: bfloat16 [16, 8192, 512], P('head', 'ctx')
The draws below stay inside these ranges and needn't reach their ends.
Inputs may be any that keep to these rules, and one draw needn't show every extreme that they name: `span_order`: a permutation; the stored spans 2 d and 2 d + 1 hold sequence spans whose numbers add up to 127. logsumexp is the log of the sum over allowed keys of all cycle steps of exp of the scaled scores of query and key as given. `query`: independent entries of order one. `key`: independent entries of order one.
All inputs are finite; a program needn't handle non-finite values.
Results may differ from the reference program's by a relative error of at most 0.0095.
Values may be sent and summed in bfloat16 or wider, within the bound.
A program may use at most 32 MiB of HBM per device.

```python
import jax
import jax.numpy as jnp
from jax import lax

HEADS = 16
KV_HEADS = 4
HEAD_DIM = 128
TOK_DEV = 128
CYCLE_STEPS = 3
SEQS = 16
LENGTH = 8192
SPANS = 128
N_CTX = 64


def shared_fields(key):
    first = jax.random.fold_in(key, 101)
    second = jax.random.fold_in(key, 202)
    raw_query = jax.random.normal(first, (SEQS, LENGTH, HEADS * HEAD_DIM), jnp.float32)
    raw_key = jax.random.normal(second, (SEQS, LENGTH, KV_HEADS * HEAD_DIM), jnp.float32)
    return (raw_query, raw_key)


def draw_span_order(key, part):
    shard_count = SPANS // 2
    early = jax.random.permutation(jax.random.fold_in(key, 303), shard_count).astype(jnp.int32)
    late = SPANS - 1 - early
    flips = jax.random.randint(jax.random.fold_in(key, 404), (shard_count,), 0, 2).astype(jnp.int32)
    leading = jnp.where(flips == 1, late, early)
    trailing = jnp.where(flips == 1, early, late)
    return jnp.stack((leading, trailing), axis=1).reshape(SPANS).astype(jnp.int32)


def draw_query(key, part):
    return shared_fields(key)[0].astype(jnp.bfloat16)


def draw_key(key, part):
    return shared_fields(key)[1].astype(jnp.bfloat16)


def draw_logsumexp(key, part):
    raw_query, raw_key = shared_fields(key)
    query_half = lax.optimization_barrier(raw_query.astype(jnp.bfloat16))
    key_half = lax.optimization_barrier(raw_key.astype(jnp.bfloat16))
    shard_count = SPANS // 2
    q_five = query_half.astype(jnp.float32).reshape(SEQS, shard_count, TOK_DEV, HEADS, HEAD_DIM)
    k_five = key_half.astype(jnp.float32).reshape(SEQS, shard_count, TOK_DEV, KV_HEADS, HEAD_DIM)
    order = draw_span_order(key, part)
    span_rows = TOK_DEV // 2
    offsets = jnp.arange(span_rows, dtype=jnp.int32)
    positions = (order[:, None] * span_rows + offsets[None, :]).reshape(shard_count, TOK_DEV)
    score_scale = HEAD_DIM ** (-0.5)
    group = HEADS // KV_HEADS

    def one_head(head_index):
        query_head = lax.dynamic_index_in_dim(q_five, head_index, 3, keepdims=False)
        key_head = lax.dynamic_index_in_dim(k_five, head_index // group, 3, keepdims=False)
        blocks = []
        for step in range(CYCLE_STEPS):
            keys_here = jnp.roll(key_head, step, axis=1)
            key_pos = jnp.roll(positions, step, axis=0)
            allowed = key_pos[:, None, :] <= positions[:, :, None]
            scores = jnp.einsum('scqd,sckd->scqk', query_head, keys_here, precision=lax.Precision.HIGHEST) * score_scale
            blocks.append(jnp.where(allowed[None], scores, -jnp.inf))
        return jax.nn.logsumexp(jnp.concatenate(blocks, axis=3), axis=3)
    totals = lax.map(one_head, jnp.arange(HEADS, dtype=jnp.int32))
    return jnp.transpose(totals, (1, 2, 3, 0)).reshape(SEQS, LENGTH, HEADS).astype(jnp.float32)


def block_levels(own_key, extent, pieces, low, top_value):
    gain, own = 1.0, jax.random.fold_in(own_key, 6)
    for position, shards_of in pieces:
        heights = jnp.exp(jax.random.uniform(jax.random.fold_in(own, position), (shards_of,), jnp.float32, low / len(pieces), top_value / len(pieces)))
        gain = gain * jnp.repeat(heights, extent[position] // shards_of).reshape([-1 if axis == position else 1 for axis in range(len(extent))])
    return gain


def centred(stream_key, dims, scale, bound, cuts=(), kind=jnp.bfloat16):
    drawn = jax.random.normal(stream_key, dims, jnp.float32) * scale
    if len(cuts) > 0:
        drawn = block_levels(stream_key, dims, cuts, -0.22, 0.18) * drawn
    return jnp.clip(drawn, min=-bound, max=bound).astype(kind)


def setup_inputs(seed: int = 0) -> dict:
    splits = jax.random.split(jax.random.key(seed), 8)
    return {
        "query": draw_query(jax.random.fold_in(splits[7], 71), 0),
        "key": draw_key(jax.random.fold_in(splits[7], 71), 0),
        "value": centred(splits[2], (SEQS, LENGTH, KV_HEADS * HEAD_DIM), 1.0, 6.0, ((0, 16), (1, 64))),
        "attn_out": centred(splits[3], (SEQS, LENGTH, HEADS * HEAD_DIM), 1.0, 6.0, ((1, 64), (2, 16))),
        "grad_out": centred(splits[4], (SEQS, LENGTH, HEADS * HEAD_DIM), 4.0, 24.0, ((0, 16), (1, 64))),
        "logsumexp": draw_logsumexp(jax.random.fold_in(splits[7], 71), 0),
        "span_order": draw_span_order(jax.random.fold_in(splits[7], 71), 0),
    }


def reference(query, key, value, attn_out, grad_out, logsumexp, span_order):
    span_rows = TOK_DEV // 2
    offsets = jnp.arange(span_rows, dtype=jnp.int32)
    positions = (span_order[:, None] * span_rows + offsets[None, :]).reshape(N_CTX, TOK_DEV)
    score_scale = HEAD_DIM ** -0.5
    group = HEADS // KV_HEADS
    q_five = query.reshape(SEQS, N_CTX, TOK_DEV, HEADS, HEAD_DIM)
    g_five = grad_out.reshape(SEQS, N_CTX, TOK_DEV, HEADS, HEAD_DIM)
    o_five = attn_out.reshape(SEQS, N_CTX, TOK_DEV, HEADS, HEAD_DIM)
    k_five = key.reshape(SEQS, N_CTX, TOK_DEV, KV_HEADS, HEAD_DIM)
    v_five = value.reshape(SEQS, N_CTX, TOK_DEV, KV_HEADS, HEAD_DIM)
    lse_four = logsumexp.reshape(SEQS, N_CTX, TOK_DEV, HEADS)
    delta_four = jnp.sum(o_five.astype(jnp.float32) * g_five.astype(jnp.float32), axis=4)

    def one_head(head_index):
        kv_index = head_index // group
        query_head = lax.dynamic_index_in_dim(q_five, head_index, 3, keepdims=False).astype(jnp.float32)
        upstream = lax.dynamic_index_in_dim(g_five, head_index, 3, keepdims=False).astype(jnp.float32)
        key_head = lax.dynamic_index_in_dim(k_five, kv_index, 3, keepdims=False)
        value_head = lax.dynamic_index_in_dim(v_five, kv_index, 3, keepdims=False)
        lse_head = lax.dynamic_index_in_dim(lse_four, head_index, 3, keepdims=False)
        delta_head = lax.dynamic_index_in_dim(delta_four, head_index, 3, keepdims=False)
        query_acc = jnp.zeros((SEQS, N_CTX, TOK_DEV, HEAD_DIM), jnp.float32)
        key_acc = jnp.zeros((SEQS, N_CTX, TOK_DEV, HEAD_DIM), jnp.float32)
        value_acc = jnp.zeros((SEQS, N_CTX, TOK_DEV, HEAD_DIM), jnp.float32)
        for step in range(CYCLE_STEPS):
            keys_here = jnp.roll(key_head, step, axis=1).astype(jnp.float32)
            values_here = jnp.roll(value_head, step, axis=1).astype(jnp.float32)
            key_pos = jnp.roll(positions, step, axis=0)
            allowed = key_pos[:, None, :] <= positions[:, :, None]
            scores = jnp.einsum("scqd,sckd->scqk", query_head, keys_here)
            attn_probs = jnp.exp(jnp.where(allowed[None], scores * score_scale - lse_head[..., None], -jnp.inf))
            dprobs = jnp.einsum("scqd,sckd->scqk", upstream, values_here)
            dscores = (attn_probs * (dprobs - delta_head[..., None])).astype(jnp.bfloat16)
            query_acc = query_acc + jnp.einsum("scqk,sckd->scqd", dscores.astype(jnp.float32), keys_here)
            key_term = (jnp.einsum("scqk,scqd->sckd", dscores.astype(jnp.float32), query_head) * score_scale).astype(jnp.bfloat16)
            value_term = jnp.einsum("scqk,scqd->sckd", attn_probs.astype(jnp.bfloat16).astype(jnp.float32), upstream).astype(jnp.bfloat16)
            key_acc = key_acc + jnp.roll(key_term.astype(jnp.float32), -step, axis=1)
            value_acc = value_acc + jnp.roll(value_term.astype(jnp.float32), -step, axis=1)
        return (query_acc * score_scale).astype(jnp.bfloat16), key_acc.astype(jnp.bfloat16), value_acc.astype(jnp.bfloat16)

    query_grad, key_grad, value_grad = lax.map(one_head, jnp.arange(HEADS, dtype=jnp.int32))
    grad_query = jnp.transpose(query_grad, (1, 2, 3, 0, 4)).reshape(SEQS, LENGTH, HEADS * HEAD_DIM)
    key_sum = key_grad.reshape(KV_HEADS, group, SEQS, N_CTX, TOK_DEV, HEAD_DIM).astype(jnp.float32).sum(axis=1).astype(jnp.bfloat16)
    value_sum = value_grad.reshape(KV_HEADS, group, SEQS, N_CTX, TOK_DEV, HEAD_DIM).astype(jnp.float32).sum(axis=1).astype(jnp.bfloat16)
    grad_key = jnp.transpose(key_sum, (1, 2, 3, 0, 4)).reshape(SEQS, LENGTH, KV_HEADS * HEAD_DIM)
    grad_value = jnp.transpose(value_sum, (1, 2, 3, 0, 4)).reshape(SEQS, LENGTH, KV_HEADS * HEAD_DIM)
    return (grad_query, grad_key, grad_value)
```

```python
import jax
import jax.numpy as jnp
from jax import lax
from jax.sharding import PartitionSpec as P

HEADS = 16
KV_HEADS = 4
HEAD_DIM = 128
CYCLE_STEPS = 3


def passed_along(value, axis, steps):
    count = lax.axis_size(axis)
    pairs = [(source, (source + steps) % count) for source in range(count)]
    return lax.ppermute(value, axis, pairs)


def shards(query, key, value, attn_out, grad_out, logsumexp, span_order):
    cycle_size = lax.axis_size("ctx")
    here = lax.axis_index("ctx")
    seq_count = query.shape[0]
    tok_rows = query.shape[1]
    span_rows = tok_rows // 2
    group = HEADS // KV_HEADS
    score_scale = HEAD_DIM ** (-0.5)
    offsets = jnp.arange(span_rows, dtype=jnp.int32)

    def shard_positions(shard):
        starts = lax.dynamic_slice_in_dim(span_order, 2 * shard, 2) * span_rows
        return (starts[:, None] + offsets[None, :]).reshape(tok_rows)

    own_kv = jnp.stack((key, value))
    kv_ahead = [passed_along(own_kv, "ctx", step) for step in range(1, CYCLE_STEPS)]

    outputs = lax.all_to_all(attn_out, "head", split_axis=0, concat_axis=2, tiled=True)
    lse_rows = lax.all_to_all(logsumexp, "head", split_axis=0, concat_axis=2, tiled=True)

    q5 = query.reshape(seq_count, tok_rows, KV_HEADS, group, HEAD_DIM)
    g5 = grad_out.reshape(seq_count, tok_rows, KV_HEADS, group, HEAD_DIM)
    o5 = outputs.reshape(seq_count, tok_rows, KV_HEADS, group, HEAD_DIM)
    delta_rows = jnp.sum(o5.astype(jnp.float32) * g5.astype(jnp.float32), axis=4)
    delta_heads = jnp.transpose(delta_rows, (0, 2, 3, 1))
    lse_heads = jnp.transpose(
        lse_rows.reshape(seq_count, tok_rows, KV_HEADS, group), (0, 2, 3, 1)
    )
    query_pos = shard_positions(here)

    def block_grads(kv_blk, key_pos):
        keys_here = kv_blk[0].reshape(seq_count, tok_rows, KV_HEADS, HEAD_DIM)
        values_here = kv_blk[1].reshape(seq_count, tok_rows, KV_HEADS, HEAD_DIM)
        scores = jnp.einsum(
            "sqgrd,skgd->sgrqk", q5, keys_here, preferred_element_type=jnp.float32
        )
        allowed = key_pos[None, :] <= query_pos[:, None]
        attn_probs = jnp.exp(
            jnp.where(allowed, scores * score_scale - lse_heads[..., None], -jnp.inf)
        )
        dprobs = jnp.einsum(
            "sqgrd,skgd->sgrqk", g5, values_here, preferred_element_type=jnp.float32
        )
        dscores = (attn_probs * (dprobs - delta_heads[..., None])).astype(jnp.bfloat16)
        query_part = jnp.einsum(
            "sgrqk,skgd->sqgrd", dscores, keys_here, preferred_element_type=jnp.float32
        )
        key_part = (
            jnp.einsum("sgrqk,sqgrd->skgd", dscores, q5, preferred_element_type=jnp.float32)
            * score_scale
        )
        value_part = jnp.einsum(
            "sgrqk,sqgrd->skgd",
            attn_probs.astype(jnp.bfloat16),
            g5,
            preferred_element_type=jnp.float32,
        )
        flat = (seq_count, tok_rows, KV_HEADS * HEAD_DIM)
        return query_part, key_part.reshape(flat), value_part.reshape(flat)

    query_sum, key_sum, value_sum = block_grads(own_kv, query_pos)
    for step in range(1, CYCLE_STEPS):
        source = (here - step) % cycle_size
        part_query, part_key, part_value = block_grads(kv_ahead[step - 1], shard_positions(source))
        query_sum = query_sum + part_query
        returned = passed_along(
            jnp.stack((part_key, part_value)).astype(jnp.bfloat16), "ctx", -step
        )
        key_sum = key_sum + returned[0].astype(jnp.float32)
        value_sum = value_sum + returned[1].astype(jnp.float32)
    query_grad = (query_sum * score_scale).astype(jnp.bfloat16).reshape(query.shape)
    return (query_grad, key_sum.astype(jnp.bfloat16), value_sum.astype(jnp.bfloat16))


def solution(mesh):
    in_specs = (
        P("head", "ctx", None),
        P("head", "ctx", None),
        P("head", "ctx", None),
        P(None, "ctx", "head"),
        P("head", "ctx", None),
        P(None, "ctx", "head"),
        P(),
    )
    out_specs = (P("head", "ctx", None), P("head", "ctx", None), P("head", "ctx", None))
    return jax.shard_map(shards, mesh=mesh, in_specs=in_specs, out_specs=out_specs, check_vma=False)
```

```python
import jax
import jax.numpy as jnp
from jax import lax
from jax.sharding import PartitionSpec as P

HEADS = 16
KV_HEADS = 4
HEAD_DIM = 128
CYCLE_STEPS = 3


def passed_along(value, axis, steps):
    count = lax.axis_size(axis)
    pairs = [(source, (source + steps) % count) for source in range(count)]
    return lax.ppermute(value, axis, pairs)


def shards(query, key, value, attn_out, grad_out, logsumexp, span_order):
    cycle_size = lax.axis_size("ctx")
    here = lax.axis_index("ctx")
    seq_count = query.shape[0]
    tok_rows = query.shape[1]
    span_rows = tok_rows // 2
    group = HEADS // KV_HEADS
    score_scale = HEAD_DIM ** (-0.5)
    offsets = jnp.arange(span_rows, dtype=jnp.int32)

    def shard_positions(shard):
        starts = lax.dynamic_slice_in_dim(span_order, 2 * shard, 2) * span_rows
        return (starts[:, None] + offsets[None, :]).reshape(tok_rows)

    own_kv = jnp.stack((key, value))
    kv_ahead = [passed_along(own_kv, "ctx", step) for step in range(1, CYCLE_STEPS)]

    lse_t = jnp.transpose(logsumexp, (0, 2, 1)).reshape(logsumexp.shape[0], 1, -1)
    lse_hi = lax.reduce_precision(lse_t, exponent_bits=8, mantissa_bits=7)
    lse_r1 = lse_t - lse_hi
    lse_mid = lax.reduce_precision(lse_r1, exponent_bits=8, mantissa_bits=7)
    lse_lo = lse_r1 - lse_mid
    packed = jnp.concatenate(
        (attn_out, lse_hi.astype(jnp.bfloat16), lse_mid.astype(jnp.bfloat16),
         lse_lo.astype(jnp.bfloat16)),
        axis=1,
    )
    moved = lax.all_to_all(packed, "head", split_axis=0, concat_axis=2, tiled=True)
    outputs = moved[:, :tok_rows, :]
    lse_parts = moved[:, tok_rows:, :].astype(jnp.float32)
    lse_sum = (lse_parts[:, 0] + lse_parts[:, 1]) + lse_parts[:, 2]

    q5 = query.reshape(seq_count, tok_rows, KV_HEADS, group, HEAD_DIM)
    g5 = grad_out.reshape(seq_count, tok_rows, KV_HEADS, group, HEAD_DIM)
    o5 = outputs.reshape(seq_count, tok_rows, KV_HEADS, group, HEAD_DIM)
    delta_rows = jnp.sum(o5.astype(jnp.float32) * g5.astype(jnp.float32), axis=4)
    delta_heads = jnp.transpose(delta_rows, (0, 2, 3, 1))
    lse_heads = lse_sum.reshape(seq_count, KV_HEADS, group, tok_rows)
    query_pos = shard_positions(here)

    def block_grads(kv_blk, key_pos):
        keys_here = kv_blk[0].reshape(seq_count, tok_rows, KV_HEADS, HEAD_DIM)
        values_here = kv_blk[1].reshape(seq_count, tok_rows, KV_HEADS, HEAD_DIM)
        scores = jnp.einsum(
            "sqgrd,skgd->sgrqk", q5, keys_here, preferred_element_type=jnp.float32
        )
        allowed = key_pos[None, :] <= query_pos[:, None]
        attn_probs = jnp.exp(
            jnp.where(allowed, scores * score_scale - lse_heads[..., None], -jnp.inf)
        )
        dprobs = jnp.einsum(
            "sqgrd,skgd->sgrqk", g5, values_here, preferred_element_type=jnp.float32
        )
        dscores = (attn_probs * (dprobs - delta_heads[..., None])).astype(jnp.bfloat16)
        query_part = jnp.einsum(
            "sgrqk,skgd->sqgrd", dscores, keys_here, preferred_element_type=jnp.float32
        )
        key_part = (
            jnp.einsum("sgrqk,sqgrd->skgd", dscores, q5, preferred_element_type=jnp.float32)
            * score_scale
        )
        value_part = jnp.einsum(
            "sgrqk,sqgrd->skgd",
            attn_probs.astype(jnp.bfloat16),
            g5,
            preferred_element_type=jnp.float32,
        )
        flat = (seq_count, tok_rows, KV_HEADS * HEAD_DIM)
        return query_part, key_part.reshape(flat), value_part.reshape(flat)

    query_sum, key_sum, value_sum = block_grads(own_kv, query_pos)
    for step in range(1, CYCLE_STEPS):
        source = (here - step) % cycle_size
        part_query, part_key, part_value = block_grads(kv_ahead[step - 1], shard_positions(source))
        query_sum = query_sum + part_query
        returned = passed_along(
            jnp.stack((part_key, part_value)).astype(jnp.bfloat16), "ctx", -step
        )
        key_sum = key_sum + returned[0].astype(jnp.float32)
        value_sum = value_sum + returned[1].astype(jnp.float32)
    query_grad = (query_sum * score_scale).astype(jnp.bfloat16).reshape(query.shape)
    return (query_grad, key_sum.astype(jnp.bfloat16), value_sum.astype(jnp.bfloat16))


def solution(mesh):
    in_specs = (
        P("head", "ctx", None),
        P("head", "ctx", None),
        P("head", "ctx", None),
        P(None, "ctx", "head"),
        P("head", "ctx", None),
        P(None, "ctx", "head"),
        P(),
    )
    out_specs = (P("head", "ctx", None), P("head", "ctx", None), P("head", "ctx", None))
    return jax.shard_map(shards, mesh=mesh, in_specs=in_specs, out_specs=out_specs, check_vma=False)
```

```python
import jax
import jax.numpy as jnp
from jax import lax
from jax.sharding import PartitionSpec as P

HEADS = 16
KV_HEADS = 4
HEAD_DIM = 128
CYCLE_STEPS = 3


def passed_along(value, axis, steps):
    count = lax.axis_size(axis)
    pairs = [(source, (source + steps) % count) for source in range(count)]
    return lax.ppermute(value, axis, pairs)


def shards(query, key, value, attn_out, grad_out, logsumexp, span_order):
    cycle_size = lax.axis_size("ctx")
    here = lax.axis_index("ctx")
    seq_count = query.shape[0]
    tok_rows = query.shape[1]
    span_rows = tok_rows // 2
    group = HEADS // KV_HEADS
    score_scale = HEAD_DIM ** (-0.5)
    offsets = jnp.arange(span_rows, dtype=jnp.int32)

    def shard_positions(shard):
        starts = lax.dynamic_slice_in_dim(span_order, 2 * shard, 2) * span_rows
        return (starts[:, None] + offsets[None, :]).reshape(tok_rows)

    own_kv = jnp.stack((key, value))
    kv_ahead = [passed_along(own_kv, "ctx", step) for step in range(1, CYCLE_STEPS)]

    outputs = lax.all_to_all(attn_out, "head", split_axis=0, concat_axis=2, tiled=True)

    q5 = query.reshape(seq_count, tok_rows, KV_HEADS, group, HEAD_DIM)
    g5 = grad_out.reshape(seq_count, tok_rows, KV_HEADS, group, HEAD_DIM)
    o5 = outputs.reshape(seq_count, tok_rows, KV_HEADS, group, HEAD_DIM)
    delta_rows = jnp.sum(o5.astype(jnp.float32) * g5.astype(jnp.float32), axis=4)
    delta_heads = jnp.transpose(delta_rows, (0, 2, 3, 1))
    query_pos = shard_positions(here)

    def scaled_scores(kv_blk, key_pos):
        keys_here = kv_blk[0].reshape(seq_count, tok_rows, KV_HEADS, HEAD_DIM)
        scores = jnp.einsum(
            "sqgrd,skgd->sgrqk", q5, keys_here, preferred_element_type=jnp.float32
        )
        allowed = key_pos[None, :] <= query_pos[:, None]
        return jnp.where(allowed, scores * score_scale, -jnp.inf)

    def block_grads(kv_blk, masked, lse_heads):
        keys_here = kv_blk[0].reshape(seq_count, tok_rows, KV_HEADS, HEAD_DIM)
        values_here = kv_blk[1].reshape(seq_count, tok_rows, KV_HEADS, HEAD_DIM)
        attn_probs = jnp.exp(masked - lse_heads[..., None])
        dprobs = jnp.einsum(
            "sqgrd,skgd->sgrqk", g5, values_here, preferred_element_type=jnp.float32
        )
        dscores = (attn_probs * (dprobs - delta_heads[..., None])).astype(jnp.bfloat16)
        query_part = jnp.einsum(
            "sgrqk,skgd->sqgrd", dscores, keys_here, preferred_element_type=jnp.float32
        )
        key_part = (
            jnp.einsum("sgrqk,sqgrd->skgd", dscores, q5, preferred_element_type=jnp.float32)
            * score_scale
        )
        value_part = jnp.einsum(
            "sgrqk,sqgrd->skgd",
            attn_probs.astype(jnp.bfloat16),
            g5,
            preferred_element_type=jnp.float32,
        )
        flat = (seq_count, tok_rows, KV_HEADS * HEAD_DIM)
        return query_part, key_part.reshape(flat), value_part.reshape(flat)

    blocks = [own_kv] + kv_ahead
    masked = [
        scaled_scores(blocks[step], shard_positions((here - step) % cycle_size))
        for step in range(CYCLE_STEPS)
    ]
    row_max = masked[0].max(axis=-1)
    for step in range(1, CYCLE_STEPS):
        row_max = jnp.maximum(row_max, masked[step].max(axis=-1))
    row_sum = sum(jnp.exp(m - row_max[..., None]).sum(axis=-1) for m in masked)
    lse_heads = row_max + jnp.log(row_sum)

    query_sum, key_sum, value_sum = block_grads(own_kv, masked[0], lse_heads)
    for step in range(1, CYCLE_STEPS):
        part_query, part_key, part_value = block_grads(blocks[step], masked[step], lse_heads)
        query_sum = query_sum + part_query
        returned = passed_along(
            jnp.stack((part_key, part_value)).astype(jnp.bfloat16), "ctx", -step
        )
        key_sum = key_sum + returned[0].astype(jnp.float32)
        value_sum = value_sum + returned[1].astype(jnp.float32)
    query_grad = (query_sum * score_scale).astype(jnp.bfloat16).reshape(query.shape)
    return (query_grad, key_sum.astype(jnp.bfloat16), value_sum.astype(jnp.bfloat16))


def solution(mesh):
    in_specs = (
        P("head", "ctx", None),
        P("head", "ctx", None),
        P("head", "ctx", None),
        P(None, "ctx", "head"),
        P("head", "ctx", None),
        P(None, "ctx", "head"),
        P(),
    )
    out_specs = (P("head", "ctx", None), P("head", "ctx", None), P("head", "ctx", None))
    return jax.shard_map(shards, mesh=mesh, in_specs=in_specs, out_specs=out_specs, check_vma=False)
```

```python
import jax
import jax.numpy as jnp
from jax import lax
from jax.sharding import PartitionSpec as P

HEADS = 16
KV_HEADS = 4
HEAD_DIM = 128
CYCLE_STEPS = 3


def passed_along(value, axis, steps):
    count = lax.axis_size(axis)
    pairs = [(source, (source + steps) % count) for source in range(count)]
    return lax.ppermute(value, axis, pairs)


def shards(query, key, value, attn_out, grad_out, logsumexp, span_order):
    cycle_size = lax.axis_size("ctx")
    here = lax.axis_index("ctx")
    seq_count = query.shape[0]
    tok_rows = query.shape[1]
    span_rows = tok_rows // 2
    group = HEADS // KV_HEADS
    score_scale = HEAD_DIM ** (-0.5)
    offsets = jnp.arange(span_rows, dtype=jnp.int32)

    def shard_positions(shard):
        starts = lax.dynamic_slice_in_dim(span_order, 2 * shard, 2) * span_rows
        return (starts[:, None] + offsets[None, :]).reshape(tok_rows)

    own_kv = jnp.stack((key, value))
    kv_ahead = [passed_along(own_kv, "ctx", step) for step in range(1, CYCLE_STEPS)]

    outputs = lax.all_to_all(attn_out, "head", split_axis=0, concat_axis=2, tiled=True)

    q5 = query.reshape(seq_count, tok_rows, KV_HEADS, group, HEAD_DIM)
    g5 = grad_out.reshape(seq_count, tok_rows, KV_HEADS, group, HEAD_DIM)
    o5 = outputs.reshape(seq_count, tok_rows, KV_HEADS, group, HEAD_DIM)
    delta_rows = jnp.sum(o5.astype(jnp.float32) * g5.astype(jnp.float32), axis=4)
    delta_heads = jnp.transpose(delta_rows, (0, 2, 3, 1))
    query_pos = shard_positions(here)

    def scaled_scores(kv_blk, key_pos):
        keys_here = kv_blk[0].reshape(seq_count, tok_rows, KV_HEADS, HEAD_DIM)
        scores = jnp.einsum(
            "sqgrd,skgd->sgrqk", q5, keys_here, preferred_element_type=jnp.float32
        )
        allowed = key_pos[None, :] <= query_pos[:, None]
        return jnp.where(allowed, scores * score_scale, -jnp.inf)

    def block_grads(kv_blk, masked, lse_heads):
        keys_here = kv_blk[0].reshape(seq_count, tok_rows, KV_HEADS, HEAD_DIM)
        values_here = kv_blk[1].reshape(seq_count, tok_rows, KV_HEADS, HEAD_DIM)
        attn_probs = jnp.exp(masked - lse_heads[..., None])
        dprobs = jnp.einsum(
            "sqgrd,skgd->sgrqk", g5, values_here, preferred_element_type=jnp.float32
        )
        dscores = (attn_probs * (dprobs - delta_heads[..., None])).astype(jnp.bfloat16)
        query_part = jnp.einsum(
            "sgrqk,skgd->sqgrd", dscores, keys_here, preferred_element_type=jnp.float32
        )
        key_part = (
            jnp.einsum("sgrqk,sqgrd->sgdk", dscores, q5, preferred_element_type=jnp.float32)
            * score_scale
        )
        value_part = jnp.einsum(
            "sgrqk,sqgrd->sgdk",
            attn_probs.astype(jnp.bfloat16),
            g5,
            preferred_element_type=jnp.float32,
        )
        return query_part, key_part, value_part

    blocks = [own_kv] + kv_ahead
    masked = [
        scaled_scores(blocks[step], shard_positions((here - step) % cycle_size))
        for step in range(CYCLE_STEPS)
    ]
    row_max = masked[0].max(axis=-1)
    for step in range(1, CYCLE_STEPS):
        row_max = jnp.maximum(row_max, masked[step].max(axis=-1))
    row_sum = sum(jnp.exp(m - row_max[..., None]).sum(axis=-1) for m in masked)
    lse_heads = row_max + jnp.log(row_sum)

    query_sum, key_sum, value_sum = block_grads(own_kv, masked[0], lse_heads)
    for step in range(1, CYCLE_STEPS):
        part_query, part_key, part_value = block_grads(blocks[step], masked[step], lse_heads)
        query_sum = query_sum + part_query
        returned = passed_along(
            jnp.stack((part_key, part_value)).astype(jnp.bfloat16), "ctx", -step
        )
        key_sum = key_sum + returned[0].astype(jnp.float32)
        value_sum = value_sum + returned[1].astype(jnp.float32)
    query_grad = (query_sum * score_scale).astype(jnp.bfloat16).reshape(query.shape)
    flat = (seq_count, tok_rows, KV_HEADS * HEAD_DIM)
    key_grad = jnp.transpose(key_sum.astype(jnp.bfloat16), (0, 3, 1, 2)).reshape(flat)
    value_grad = jnp.transpose(value_sum.astype(jnp.bfloat16), (0, 3, 1, 2)).reshape(flat)
    return (query_grad, key_grad, value_grad)


def solution(mesh):
    in_specs = (
        P("head", "ctx", None),
        P("head", "ctx", None),
        P("head", "ctx", None),
        P(None, "ctx", "head"),
        P("head", "ctx", None),
        P(None, "ctx", "head"),
        P(),
    )
    out_specs = (P("head", "ctx", None), P("head", "ctx", None), P("head", "ctx", None))
    return jax.shard_map(shards, mesh=mesh, in_specs=in_specs, out_specs=out_specs, check_vma=False)
```

```python
import jax
import jax.numpy as jnp
from jax import lax
from jax.sharding import PartitionSpec as P

HEADS = 16
KV_HEADS = 4
HEAD_DIM = 128
CYCLE_STEPS = 3


def passed_along(value, axis, steps):
    count = lax.axis_size(axis)
    pairs = [(source, (source + steps) % count) for source in range(count)]
    return lax.ppermute(value, axis, pairs)


def shards(query, key, value, attn_out, grad_out, logsumexp, span_order):
    cycle_size = lax.axis_size("ctx")
    here = lax.axis_index("ctx")
    seq_count = query.shape[0]
    tok_rows = query.shape[1]
    span_rows = tok_rows // 2
    group = HEADS // KV_HEADS
    score_scale = HEAD_DIM ** (-0.5)
    offsets = jnp.arange(span_rows, dtype=jnp.int32)

    def shard_positions(shard):
        starts = lax.dynamic_slice_in_dim(span_order, 2 * shard, 2) * span_rows
        return (starts[:, None] + offsets[None, :]).reshape(tok_rows)

    own_kv = jnp.stack((key, value))
    kv_ahead = [passed_along(own_kv, "ctx", step) for step in range(1, CYCLE_STEPS)]

    outputs = lax.all_to_all(attn_out, "head", split_axis=0, concat_axis=2, tiled=True)

    q5 = query.reshape(seq_count, tok_rows, KV_HEADS, group, HEAD_DIM)
    g5 = grad_out.reshape(seq_count, tok_rows, KV_HEADS, group, HEAD_DIM)
    o5 = outputs.reshape(seq_count, tok_rows, KV_HEADS, group, HEAD_DIM)
    delta_rows = jnp.sum(o5.astype(jnp.float32) * g5.astype(jnp.float32), axis=4)
    delta_heads = jnp.transpose(delta_rows, (0, 2, 3, 1))
    query_pos = shard_positions(here)

    def scaled_scores(kv_blk, key_pos):
        keys_here = kv_blk[0].reshape(seq_count, tok_rows, KV_HEADS, HEAD_DIM)
        scores = jnp.einsum(
            "sqgrd,skgd->sgrqk", q5, keys_here, preferred_element_type=jnp.float32
        )
        allowed = key_pos[None, :] <= query_pos[:, None]
        return jnp.where(allowed, scores * score_scale, -jnp.inf)

    def block_grads(kv_blk, masked, lse_heads):
        keys_here = kv_blk[0].reshape(seq_count, tok_rows, KV_HEADS, HEAD_DIM)
        values_here = kv_blk[1].reshape(seq_count, tok_rows, KV_HEADS, HEAD_DIM)
        attn_probs = jnp.exp(masked - lse_heads[..., None])
        dprobs = jnp.einsum(
            "sqgrd,skgd->sgrqk", g5, values_here, preferred_element_type=jnp.float32
        )
        dscores = (attn_probs * (dprobs - delta_heads[..., None])).astype(jnp.bfloat16)
        query_part = jnp.einsum(
            "sgrqk,skgd->sqgrd", dscores, keys_here, preferred_element_type=jnp.float32
        )
        key_part = (
            jnp.einsum("sgrqk,sqgrd->sgdk", dscores, q5, preferred_element_type=jnp.float32)
            * score_scale
        )
        value_part = jnp.einsum(
            "sgrqk,sqgrd->sgdk",
            attn_probs.astype(jnp.bfloat16),
            g5,
            preferred_element_type=jnp.float32,
        )
        return query_part, key_part, value_part

    blocks = [own_kv] + kv_ahead
    masked = [
        scaled_scores(blocks[step], shard_positions((here - step) % cycle_size))
        for step in range(CYCLE_STEPS)
    ]
    row_max = masked[0].max(axis=-1)
    for step in range(1, CYCLE_STEPS):
        row_max = jnp.maximum(row_max, masked[step].max(axis=-1))
    row_sum = sum(jnp.exp(m - row_max[..., None]).sum(axis=-1) for m in masked)
    lse_heads = row_max + jnp.log(row_sum)

    query_sum, key_sum, value_sum = block_grads(own_kv, masked[0], lse_heads)
    for step in range(1, CYCLE_STEPS):
        part_query, part_key, part_value = block_grads(blocks[step], masked[step], lse_heads)
        query_sum = query_sum + part_query
        value_back = passed_along(part_value.astype(jnp.bfloat16), "ctx", -step)
        key_back = passed_along(part_key.astype(jnp.bfloat16), "ctx", -step)
        key_sum = key_sum + key_back.astype(jnp.float32)
        value_sum = value_sum + value_back.astype(jnp.float32)
    query_grad = (query_sum * score_scale).astype(jnp.bfloat16).reshape(query.shape)
    flat = (seq_count, tok_rows, KV_HEADS * HEAD_DIM)
    key_grad = jnp.transpose(key_sum.astype(jnp.bfloat16), (0, 3, 1, 2)).reshape(flat)
    value_grad = jnp.transpose(value_sum.astype(jnp.bfloat16), (0, 3, 1, 2)).reshape(flat)
    return (query_grad, key_grad, value_grad)


def solution(mesh):
    in_specs = (
        P("head", "ctx", None),
        P("head", "ctx", None),
        P("head", "ctx", None),
        P(None, "ctx", "head"),
        P("head", "ctx", None),
        P(None, "ctx", "head"),
        P(),
    )
    out_specs = (P("head", "ctx", None), P("head", "ctx", None), P("head", "ctx", None))
    return jax.shard_map(shards, mesh=mesh, in_specs=in_specs, out_specs=out_specs, check_vma=False)
```

```python
import jax
import jax.numpy as jnp
from jax import lax
from jax.sharding import PartitionSpec as P

HEADS = 16
KV_HEADS = 4
HEAD_DIM = 128
CYCLE_STEPS = 3


def passed_along(value, axis, steps):
    count = lax.axis_size(axis)
    pairs = [(source, (source + steps) % count) for source in range(count)]
    return lax.ppermute(value, axis, pairs)


def shards_body(query, key, value, attn_out, grad_out, logsumexp, span_order):
    cycle_size = lax.axis_size("ctx")
    here = lax.axis_index("ctx")
    seq_count = query.shape[0]
    tok_rows = query.shape[1]
    span_rows = tok_rows // 2
    group = HEADS // KV_HEADS
    score_scale = HEAD_DIM ** (-0.5)
    offsets = jnp.arange(span_rows, dtype=jnp.int32)

    def shard_positions(shard):
        starts = lax.dynamic_slice_in_dim(span_order, 2 * shard, 2) * span_rows
        return (starts[:, None] + offsets[None, :]).reshape(tok_rows)

    own_kv = jnp.stack((key, value))
    kv_ahead = []
    for step in range(1, CYCLE_STEPS):
        kv_ahead.append(passed_along(own_kv, "ctx", step))

    outputs = lax.all_to_all(attn_out, "head", split_axis=0, concat_axis=2, tiled=True)

    q5 = query.reshape(seq_count, tok_rows, KV_HEADS, group, HEAD_DIM)
    g5 = grad_out.reshape(seq_count, tok_rows, KV_HEADS, group, HEAD_DIM)
    o5 = outputs.reshape(seq_count, tok_rows, KV_HEADS, group, HEAD_DIM)
    delta_rows = jnp.sum(o5.astype(jnp.float32) * g5.astype(jnp.float32), axis=4)
    delta_heads = jnp.transpose(delta_rows, (0, 2, 3, 1))
    query_pos = shard_positions(here)

    def scaled_scores(kv_blk, key_pos):
        keys_here = kv_blk[0].reshape(seq_count, tok_rows, KV_HEADS, HEAD_DIM)
        scores = jnp.einsum(
            "sqgrd,skgd->sgrqk", q5, keys_here, preferred_element_type=jnp.float32
        )
        allowed = key_pos[None, :] <= query_pos[:, None]
        return jnp.where(allowed, scores * score_scale, -jnp.inf)

    def block_grads(kv_blk, masked, lse_heads):
        keys_here = kv_blk[0].reshape(seq_count, tok_rows, KV_HEADS, HEAD_DIM)
        values_here = kv_blk[1].reshape(seq_count, tok_rows, KV_HEADS, HEAD_DIM)
        attn_probs = jnp.exp(masked - lse_heads[..., None])
        dprobs = jnp.einsum(
            "sqgrd,skgd->sgrqk", g5, values_here, preferred_element_type=jnp.float32
        )
        dscores = (attn_probs * (dprobs - delta_heads[..., None])).astype(jnp.bfloat16)
        query_part = jnp.einsum(
            "sgrqk,skgd->sqgrd", dscores, keys_here, preferred_element_type=jnp.float32
        )
        key_part = (
            jnp.einsum("sgrqk,sqgrd->sgdk", dscores, q5, preferred_element_type=jnp.float32)
            * score_scale
        )
        value_part = jnp.einsum(
            "sgrqk,sqgrd->sgdk",
            attn_probs.astype(jnp.bfloat16),
            g5,
            preferred_element_type=jnp.float32,
        )
        return query_part, key_part, value_part

    blocks = [own_kv] + kv_ahead
    masked = [
        scaled_scores(blocks[step], shard_positions((here - step) % cycle_size))
        for step in range(CYCLE_STEPS)
    ]
    row_max = masked[0].max(axis=-1)
    for step in range(1, CYCLE_STEPS):
        row_max = jnp.maximum(row_max, masked[step].max(axis=-1))
    row_sum = sum(jnp.exp(m - row_max[..., None]).sum(axis=-1) for m in masked)
    lse_heads = row_max + jnp.log(row_sum)

    query_sum, key_sum, value_sum = block_grads(own_kv, masked[0], lse_heads)
    for step in range(1, CYCLE_STEPS):
        part_query, part_key, part_value = block_grads(blocks[step], masked[step], lse_heads)
        query_sum = query_sum + part_query
        value_back = passed_along(part_value.astype(jnp.bfloat16), "ctx", -step)
        key_back = passed_along(part_key.astype(jnp.bfloat16), "ctx", -step)
        key_sum = key_sum + key_back.astype(jnp.float32)
        value_sum = value_sum + value_back.astype(jnp.float32)
    query_grad = (query_sum * score_scale).astype(jnp.bfloat16).reshape(query.shape)
    flat = (seq_count, tok_rows, KV_HEADS * HEAD_DIM)
    key_grad = jnp.transpose(key_sum.astype(jnp.bfloat16), (0, 3, 1, 2)).reshape(flat)
    value_grad = jnp.transpose(value_sum.astype(jnp.bfloat16), (0, 3, 1, 2)).reshape(flat)
    return (query_grad, key_grad, value_grad)


def solution(mesh):
    in_specs = (
        P("head", "ctx", None),
        P("head", "ctx", None),
        P("head", "ctx", None),
        P(None, "ctx", "head"),
        P("head", "ctx", None),
        P(None, "ctx", "head"),
        P(),
    )
    out_specs = (P("head", "ctx", None), P("head", "ctx", None), P("head", "ctx", None))
    return jax.shard_map(shards_body, mesh=mesh, in_specs=in_specs, out_specs=out_specs, check_vma=False)
```
